256 devices in a mesh: src: 16 (over x_lo, y, core), rcv: 16 (over z, x_hi).
Axes of the slice: x: 4 (x_hi: 2, x_lo: 2; x = x_hi * 2 + x_lo), y: 4, z: 8, core: 2. Of those that a mesh axis runs over, the one named last changes fastest.
Arguments:
- recorded: bfloat16 [2, 16384, 16384], P(None, 'src', 'rcv'), may hold values from -6 to 6
- obliquity: float32 [16, 1024], replicated, may hold values from 0.01 to 0.25
- clip_level: float32 [16384], P('src'), may hold values from 0.3 to 3
Outputs:
- first_pass: bfloat16 [2, 16384, 16384], P(None, 'src', 'rcv')
- primaries: bfloat16 [2, 16384, 16384], P(None, 'src', 'rcv')
The draws below stay inside these ranges and needn't reach their ends.
All inputs are finite; a program needn't handle non-finite values.
Results may differ from the reference program's by a relative error of at most 0.0025.
Values may be sent and summed in bfloat16 or wider, within the bound.
A program may use at most 128 MiB of HBM per device.

```python
import math
import jax
import jax.numpy as jnp
from jax import lax

N = 16384
K = 256
GROUPS = 16
COLS = 1024


def shard_levels(key, extent, split, smallest, largest):
    level, own = 1.0, jax.random.fold_in(key, 6)
    for position, shards_of in split:
        heights = jnp.exp(jax.random.uniform(jax.random.fold_in(own, position), (shards_of,), jnp.float32, smallest / len(split), largest / len(split)))
        level = level * jnp.repeat(heights, extent[position] // shards_of).reshape([-1 if axis == position else 1 for axis in range(len(extent))])
    return level


def gaussian(own_key, shape, spread, bound, pieces=(), kind=jnp.bfloat16):
    drawn = jax.random.normal(own_key, shape, jnp.float32) * spread
    if len(pieces) > 0:
        drawn = shard_levels(own_key, shape, pieces, -0.22, 0.18) * drawn
    return jnp.clip(drawn, min=-bound, max=bound).astype(kind)


def setup_inputs(seed: int = 0) -> dict:
    key_list = jax.random.split(jax.random.key(seed), 4)
    recorded = gaussian(key_list[0], (2, N, N), 1.0, 6.0, ((1, 16), (2, 16)))
    obliquity = jnp.clip(jnp.exp(jax.random.uniform(key_list[1], (GROUPS, COLS), jnp.float32, math.log(0.01), math.log(0.25))), 0.01, 0.25)
    clip_level = jnp.clip(jnp.exp(math.log(3.0) - 2.3025851 * jax.random.uniform(key_list[2], (N,), jnp.float32) ** shard_levels(key_list[2], (N,), ((0, 16),), -0.2, 0.2)), 0.3, 3.0)
    return dict(recorded=recorded, obliquity=obliquity, clip_level=clip_level)


def apply_update(left_columns, recorded, right_joined, clip_level):
    block_rows = min(1024, N)
    block_total = N // block_rows
    left_joined = jnp.concatenate([left_columns[0], left_columns[1]], axis=1).astype(jnp.float32)

    def one_block(block_index):
        first_row = block_index * block_rows
        left_rows = lax.dynamic_slice_in_dim(left_joined, first_row, block_rows, 0)
        product_sum = jnp.dot(left_rows, right_joined, precision=lax.Precision.HIGHEST, preferred_element_type=jnp.float32)
        pred_real = product_sum[:, :N]
        pred_imag = product_sum[:, N:]
        clip_rows = lax.dynamic_slice_in_dim(clip_level, first_row, block_rows, 0)[:, None]
        limiter = 1.0 / jnp.sqrt(1.0 + (pred_real * pred_real + pred_imag * pred_imag) / (clip_rows * clip_rows))
        base_rows = lax.dynamic_slice_in_dim(recorded, first_row, block_rows, 1).astype(jnp.float32)
        return (base_rows - jnp.stack([pred_real * limiter, pred_imag * limiter])).astype(jnp.bfloat16)
    blocks = lax.map(one_block, jnp.arange(block_total, dtype=jnp.int32))
    return jnp.transpose(blocks, (1, 0, 2, 3)).reshape(2, N, N)

def reference(recorded, obliquity, clip_level):
    spacing = N // K
    panel = recorded[:, ::spacing, :].astype(jnp.float32)
    spectrum = jnp.fft.fft(panel[0] + 1j * panel[1], axis=-1)
    weights = jnp.transpose(obliquity).reshape(-1)
    filtered_complex = jnp.fft.ifft(spectrum * weights, axis=-1)
    filtered = jnp.stack([jnp.real(filtered_complex), jnp.imag(filtered_complex)]).astype(jnp.bfloat16)
    filtered = lax.optimization_barrier(filtered).astype(jnp.float32)
    upper = jnp.concatenate([filtered[0], filtered[1]], axis=1)
    lower = jnp.concatenate([-filtered[1], filtered[0]], axis=1)
    right_joined = jnp.concatenate([upper, lower], axis=0)
    first_pass = apply_update(recorded[:, :, ::spacing], recorded, right_joined, clip_level)
    primaries = apply_update(first_pass[:, :, ::spacing], recorded, right_joined, clip_level)
    return (first_pass, primaries)
```

```python
import functools

import jax
import jax.numpy as jnp
import numpy as np
from jax import lax
from jax.experimental import pallas as pl
from jax.experimental.pallas import tpu as pltpu
from jax.sharding import PartitionSpec as P

N = 16384
K = 256
MESH = pl.DeviceIdType.MESH
F32 = jnp.float32
BF16 = jnp.bfloat16
HIGHEST = lax.Precision.HIGHEST
NR = 16
NS = 16
ROWS = 1024
COLS = 1024
WIDE = COLS + K


def tables():
    k1 = np.arange(128)
    rho = np.arange(256)
    n1 = 8 * ((rho >> 1) & 15) + (rho >> 5)
    part = rho & 1
    theta = 2 * np.pi * ((k1[:, None] * n1[None, :]) % 128) / 128
    cos, sin = np.cos(theta), np.sin(theta)
    even = part[None, :] == 0
    m1 = np.concatenate([np.where(even, cos, sin), np.where(even, -sin, cos)], axis=0)
    m4 = np.concatenate([np.where(even, cos, sin).T, np.where(even, -sin, cos).T], axis=1)
    angle = 2 * np.pi * ((k1[:, None] * k1[None, :]) % 128) / 128
    cos, sin = np.cos(angle), np.sin(angle)
    m2 = np.block([[cos, -sin], [sin, cos]])
    m3 = np.block([[cos, sin], [-sin, cos]])
    phi = 2 * np.pi * (k1[:, None] * k1[None, :]) / N
    twiddle = np.stack([np.cos(phi), np.sin(phi)])
    return np.stack([m1, m2, m3, m4]).astype(np.float32), twiddle.astype(np.float32)


def gather_kernel(
    rec_hbm, obl_ref, dft_ref, twi_ref, left_hbm, filt_hbm,
    rec, send1, recv1, send2, recv2, lbuf, fbuf, lnat, weights,
    rec_sem, out_sem, s1_sem, r1_sem, s2_sem, r2_sem, ls_sem, lr_sem, fs_sem, fr_sem,
):
    s = lax.axis_index("src")
    r = lax.axis_index("rcv")
    z, xh = r // 2, lax.rem(r, 2)
    xl, y, c = s // 8, lax.rem(s // 2, 4), lax.rem(s, 2)

    def src_of(x, yy, core):
        return x * 8 + lax.rem(yy + 8, 4) * 2 + core

    def rcv_of(zz, x):
        return lax.rem(zz + 16, 8) * 2 + x

    def to_rcv(index):
        return (s, index)

    def to_src(index):
        return (index, r)

    peers = [to_rcv(lax.rem(r + d, NR)) for d in range(1, NR)]
    x_peer = src_of(1 - xl, y, c)
    up, down = src_of(xl, y + 1, c), src_of(xl, y - 1, c)
    mate = src_of(xl, y, 1 - c)
    peers += [to_src(i) for i in (x_peer, up, down, mate)]

    barrier = pltpu.get_barrier_semaphore()
    for peer in peers:
        pl.semaphore_signal(barrier, inc=1, device_id=peer, device_id_type=MESH)

    chunk = ROWS // 4
    loads = []
    for q in range(4):
        load = pltpu.make_async_copy(
            rec_hbm.at[:, pl.ds(q * chunk, chunk), :], rec.at[:, pl.ds(q * chunk, chunk), :], rec_sem.at[q]
        )
        load.start()
        loads.append(load)

    obl = obl_ref[...] * (1.0 / N)
    hi = obl.astype(BF16)
    rest = obl - hi.astype(F32)
    mid = rest.astype(BF16)
    low = (rest - mid.astype(F32)).astype(BF16)
    parts = jnp.concatenate([hi, mid, low], axis=0)
    column = lax.broadcasted_iota(jnp.int32, (1024, 1024), 0)
    target = lax.broadcasted_iota(jnp.int32, (1024, 1024), 1)
    permute = jnp.where(column == 8 * (target % 128) + target // 128, 1.0, 0.0).astype(BF16)
    moved = jnp.dot(parts, permute, preferred_element_type=F32)
    moved = (moved[0:16] + moved[16:32]) + moved[32:48]
    for h in range(8):
        weights[16 * h : 16 * h + 16, :] = moved[:, 128 * h : 128 * h + 128]

    lane = lax.broadcasted_iota(jnp.int32, (1024, 128), 1)
    depth = lax.broadcasted_iota(jnp.int32, (1024, 128), 0)
    pick0 = jnp.where(depth == 64 * lane, 1.0, 0.0).astype(BF16)
    pick1 = jnp.where(depth == 64 * (lane - 16), 1.0, 0.0).astype(BF16)
    pieces = []
    for q in range(4):
        loads[q].wait()
        for i in range(4 * q, 4 * q + 4):
            rows = [rec[p, 64 * i : 64 * i + 8, :].astype(F32)[0:1] for p in range(2)]
            send1[i] = jnp.concatenate(rows, axis=0).astype(BF16)
    for q in range(4):
        span = slice(q * chunk, q * chunk + chunk)
        columns = jnp.dot(rec[0, span, :], pick0, preferred_element_type=F32)
        columns += jnp.dot(rec[1, span, :], pick1, preferred_element_type=F32)
        turned = columns.T
        pieces.append(turned[0:32])
    local = jnp.concatenate(pieces, axis=1).astype(BF16)
    lbuf[r, 0] = local[0:16]
    lbuf[r, 1] = local[16:32]

    pl.semaphore_wait(barrier, len(peers))

    def remote(src, dst, send_sem, recv_sem, device):
        copy = pltpu.make_async_remote_copy(
            src_ref=src, dst_ref=dst, send_sem=send_sem, recv_sem=recv_sem, device_id=device, device_id_type=MESH
        )
        copy.start()
        return copy

    sent = []
    order = [8, 9, 7, 6, 10, 11, 5, 4, 12, 13, 3, 2, 14, 15, 1]
    for n, d in enumerate(order):
        other = lax.rem(r + d, NR)
        sent.append(remote(send1.at[other], recv1.at[r], s1_sem.at[n], r1_sem.at[r], to_rcv(other)))
    recv1[r] = send1[r]

    lcount = [0]

    def left_send(owner, h, target):
        n = lcount[0]
        lcount[0] += 1
        sent.append(remote(lbuf.at[owner, h], lbuf.at[owner, h], ls_sem.at[n], lr_sem.at[owner, h], to_rcv(target)))

    def left_wait(owner, h):
        pltpu.make_async_copy(lbuf.at[owner, h], lbuf.at[owner, h], lr_sem.at[owner, h]).wait()

    z_up, z_down = rcv_of(z + 1, xh), rcv_of(z - 1, xh)
    far = rcv_of(z, 1 - xh)
    for h in range(2):
        left_send(r, h, far)
    for h in range(2):
        left_send(r, h, z_up)
        left_send(r, h, z_down)

    def left_round(dist, x):
        for h in range(2):
            if dist < 4 or h == 0:
                left_wait(rcv_of(z - dist, x), h)
                if dist + 1 < 4 or (dist + 1 == 4 and h == 0):
                    left_send(rcv_of(z - dist, x), h, z_up)
            if dist < 4 or h == 1:
                left_wait(rcv_of(z + dist, x), h)
                if dist + 1 < 4 or (dist + 1 == 4 and h == 1):
                    left_send(rcv_of(z + dist, x), h, z_down)

    for h in range(2):
        left_wait(far, h)
        left_send(far, h, z_up)
        left_send(far, h, z_down)
    left_round(1, xh)

    for d in range(1, NR):
        other = lax.rem(r + d, NR)
        pltpu.make_async_copy(recv1.at[other], recv1.at[other], r1_sem.at[other]).wait()
    rows = recv1[...].astype(F32).reshape(32, 1024)
    x = jnp.concatenate([rows[:, 128 * j : 128 * j + 128] for j in range(8)], axis=0)
    cos, sin = twi_ref[0], twi_ref[1]
    a = jnp.dot(dft_ref[0], x, precision=HIGHEST, preferred_element_type=F32)
    ar, ai = a[0:128], a[128:256]
    b = jnp.concatenate([ar * cos + ai * sin, ai * cos - ar * sin], axis=1)
    b = jnp.dot(b, dft_ref[1], precision=HIGHEST, preferred_element_type=F32)
    w = weights[...]
    b = b * jnp.concatenate([w, w], axis=1)
    b = jnp.dot(b, dft_ref[2], precision=HIGHEST, preferred_element_type=F32)
    ur, ui = b[:, 0:128], b[:, 128:256]
    u = jnp.concatenate([ur * cos - ui * sin, ui * cos + ur * sin], axis=0)
    out = jnp.dot(dft_ref[3], u, precision=HIGHEST, preferred_element_type=F32)

    rounded = out.astype(BF16)
    rho = lax.broadcasted_iota(jnp.int32, (256, 512), 0)
    goal = lax.broadcasted_iota(jnp.int32, (256, 512), 1)
    place = (rho & 1) * 256 + 2 * (8 * ((rho >> 1) & 15) + (rho >> 5))
    sampled = None
    for e in range(2):
        choose = jnp.where(goal == place + e, 1.0, 0.0).astype(BF16)
        got = lax.dot_general(rounded, choose, (((0,), (0,)), ((), ())), preferred_element_type=F32)
        got = got[64 * e : 64 * e + 1]
        sampled = got if sampled is None else sampled + got
    sampled = jnp.concatenate([sampled[:, 0:256], sampled[:, 256:512]], axis=0)
    spread = jnp.concatenate([out[32 * j : 32 * j + 32] for j in range(8)], axis=1)
    for i in range(NR):
        send2[i] = jnp.concatenate([spread[2 * i : 2 * i + 2], sampled], axis=1).astype(BF16)

    for n, d in enumerate(order):
        other = lax.rem(r + d, NR)
        sent.append(remote(send2.at[other], recv2.at[r], s2_sem.at[n], r2_sem.at[r], to_rcv(other)))
    recv2[r] = send2[r]

    left_round(1, 1 - xh)
    left_round(2, xh)
    left_round(2, 1 - xh)

    for d in range(1, NR):
        other = lax.rem(r + d, NR)
        pltpu.make_async_copy(recv2.at[other], recv2.at[other], r2_sem.at[other]).wait()
    got = recv2[...].astype(F32)
    fbuf[s, 0] = got[:, 0, :].astype(BF16)
    fbuf[s, 1] = got[:, 1, :].astype(BF16)

    fcount = [0]

    def filt_send(owner, h, target):
        n = fcount[0]
        fcount[0] += 1
        sent.append(remote(fbuf.at[owner, h], fbuf.at[owner, h], fs_sem.at[n], fr_sem.at[owner, h], to_src(target)))

    def filt_wait(owner, h):
        pltpu.make_async_copy(fbuf.at[owner, h], fbuf.at[owner, h], fr_sem.at[owner, h]).wait()

    for h in range(2):
        filt_send(s, h, x_peer)
    for h in range(2):
        filt_send(s, h, up)
        filt_send(s, h, down)
        filt_send(s, h, mate)
    left_round(3, xh)
    left_round(3, 1 - xh)
    for h in range(2):
        filt_wait(x_peer, h)
        for target in (up, down, mate):
            filt_send(x_peer, h, target)
    left_round(4, xh)
    left_round(4, 1 - xh)
    for x in (xl, 1 - xl):
        for h in range(2):
            below, above = src_of(x, y - 1, c), src_of(x, y + 1, c)
            filt_wait(below, h)
            if h == 0:
                filt_send(below, h, up)
            filt_send(below, h, mate)
            filt_wait(above, h)
            if h == 1:
                filt_send(above, h, down)
            filt_send(above, h, mate)

    for p in range(2):
        for g in range(2):
            part = lbuf[8 * g : 8 * g + 8, p].reshape(128, ROWS)
            lnat[:, 256 * p + 128 * g : 256 * p + 128 * g + 128] = part.astype(F32).T.astype(BF16)
    left_out = pltpu.make_async_copy(lnat, left_hbm, out_sem.at[0])
    left_out.start()

    for x in (xl, 1 - xl):
        for h in range(2):
            opposite = src_of(x, y + 2, c)
            filt_wait(opposite, h)
            filt_send(opposite, h, mate)
    for x in range(2):
        for yy in range(4):
            for h in range(2):
                filt_wait(src_of(x, yy, 1 - c), h)
    filt_out = pltpu.make_async_copy(fbuf, filt_hbm, out_sem.at[1])
    filt_out.start()
    for copy in sent:
        copy.wait_send()
    left_out.wait()
    filt_out.wait()


def gather(recorded, obliquity):
    dft, twiddle = tables()
    vmem = pl.BlockSpec(memory_space=pltpu.VMEM)
    anywhere = pl.BlockSpec(memory_space=pl.ANY)
    dma = pltpu.SemaphoreType.DMA
    return pl.pallas_call(
        gather_kernel,
        out_shape=(
            jax.ShapeDtypeStruct((ROWS, 2 * K), BF16),
            jax.ShapeDtypeStruct((NS, 2, 16, WIDE), BF16),
        ),
        in_specs=[anywhere, vmem, vmem, vmem],
        out_specs=(anywhere, anywhere),
        scratch_shapes=[
            pltpu.VMEM((2, ROWS, COLS), BF16),
            pltpu.VMEM((NR, 2, COLS), BF16),
            pltpu.VMEM((NR, 2, COLS), BF16),
            pltpu.VMEM((NR, 2, WIDE), BF16),
            pltpu.VMEM((NR, 2, WIDE), BF16),
            pltpu.VMEM((NR, 2, 16, ROWS), BF16),
            pltpu.VMEM((NS, 2, 16, WIDE), BF16),
            pltpu.VMEM((ROWS, 2 * K), BF16),
            pltpu.VMEM((128, 128), F32),
            dma((4,)),
            dma((2,)),
            dma((NR,)),
            dma((NR,)),
            dma((NR,)),
            dma((NR,)),
            dma((32,)),
            dma((NR, 2)),
            dma((32,)),
            dma((NS, 2)),
        ],
        compiler_params=pltpu.CompilerParams(
            collective_id=0, has_side_effects=True, vmem_limit_bytes=40 * 2**20
        ),
        name="gather",
    )(recorded, obliquity, jnp.asarray(dft), jnp.asarray(twiddle))


TM = 128


def update_kernel(rec_ref, left_ref, filt_ref, clip_ref, first_ref, second_ref, right, sampled):
    step = pl.program_id(0)

    @pl.when(step == 0)
    def _():
        for p, places in ((0, (256,)), (1, (0,))):
            value = filt_ref[:, p].reshape(K, WIDE)
            for place in places:
                right[place : place + K, :] = value[:, :COLS]
                sampled[place : place + K, :] = value[:, COLS:]
            if p == 1:
                right[512:768, :] = -value[:, :COLS]
                sampled[512:768, :] = -value[:, COLS:]

    clip = jnp.broadcast_to(clip_ref[pl.ds(step, 1), :], (128, 128)).T
    scale = 1.0 / (clip * clip)
    scale = jnp.concatenate([scale, scale], axis=1)

    def limited(left, table, span):
        real = jnp.dot(left, table[256:768, span], preferred_element_type=F32)
        imag = jnp.dot(left, table[0:512, span], preferred_element_type=F32)
        limiter = lax.rsqrt(1.0 + (real * real + imag * imag) * scale)
        return real * limiter, imag * limiter

    left = left_ref[...]
    real, imag = limited(left, sampled, slice(0, 256))
    left2 = jnp.concatenate(
        [
            (left[:, 0:256].astype(F32) - real).astype(BF16),
            (left[:, 256:512].astype(F32) - imag).astype(BF16),
        ],
        axis=1,
    )
    for q in range(COLS // 256):
        span = slice(256 * q, 256 * q + 256)
        base = [rec_ref[p, :, span].astype(F32) for p in range(2)]
        for rows, out in ((left, first_ref), (left2, second_ref)):
            real, imag = limited(rows, right, span)
            out[0, :, span] = (base[0] - real).astype(BF16)
            out[1, :, span] = (base[1] - imag).astype(BF16)


def update(recorded, left, filtered, clip_level):
    block = pl.BlockSpec((2, TM, COLS), lambda i: (0, i, 0))
    once = dict(pipeline_mode=pl.Buffered(1))
    out = jax.ShapeDtypeStruct((2, ROWS, COLS), BF16)
    return pl.pallas_call(
        update_kernel,
        out_shape=(out, out),
        grid=(ROWS // TM,),
        in_specs=[
            block,
            pl.BlockSpec((TM, 2 * K), lambda i: (i, 0)),
            pl.BlockSpec((NS, 2, 16, WIDE), lambda i: (0, 0, 0, 0), **once),
            pl.BlockSpec((ROWS // 128, 128), lambda i: (0, 0), **once),
        ],
        out_specs=(block, block),
        scratch_shapes=[pltpu.VMEM((3 * K, COLS), BF16), pltpu.VMEM((3 * K, K), BF16)],
        compiler_params=pltpu.CompilerParams(vmem_limit_bytes=40 * 2**20),
        name="update",
    )(recorded, left, filtered, clip_level)


def per_device(recorded, obliquity, clip_level):
    left, filtered = gather(recorded, obliquity)
    return update(recorded, left, filtered, clip_level.reshape(ROWS // 128, 128))


def solution(mesh):
    return jax.shard_map(
        per_device,
        mesh=mesh,
        in_specs=(P(None, "src", "rcv"), P(), P("src")),
        out_specs=(P(None, "src", "rcv"), P(None, "src", "rcv")),
        check_vma=False,
    )
```

```python
import functools

import jax
import jax.numpy as jnp
import numpy as np
from jax import lax
from jax.experimental import pallas as pl
from jax.experimental.pallas import tpu as pltpu
from jax.sharding import PartitionSpec as P

N = 16384
K = 256
MESH = pl.DeviceIdType.MESH
F32 = jnp.float32
BF16 = jnp.bfloat16
HIGHEST = lax.Precision.HIGHEST
NR = 16
NS = 16
ROWS = 1024
COLS = 1024
WIDE = COLS + K


def tables():
    k1 = np.arange(128)
    rho = np.arange(256)
    n1 = 8 * ((rho >> 1) & 15) + (rho >> 5)
    part = rho & 1
    theta = 2 * np.pi * ((k1[:, None] * n1[None, :]) % 128) / 128
    cos, sin = np.cos(theta), np.sin(theta)
    even = part[None, :] == 0
    m1 = np.concatenate([np.where(even, cos, sin), np.where(even, -sin, cos)], axis=0)
    m4 = np.concatenate([np.where(even, cos, sin).T, np.where(even, -sin, cos).T], axis=1)
    angle = 2 * np.pi * ((k1[:, None] * k1[None, :]) % 128) / 128
    cos, sin = np.cos(angle), np.sin(angle)
    m2 = np.block([[cos, -sin], [sin, cos]])
    m3 = np.block([[cos, sin], [-sin, cos]])
    phi = 2 * np.pi * (k1[:, None] * k1[None, :]) / N
    twiddle = np.stack([np.cos(phi), np.sin(phi)])
    return np.stack([m1, m2, m3, m4]).astype(np.float32), twiddle.astype(np.float32)


def gather_kernel(
    rec_hbm, obl_hbm, dft_hbm, twi_hbm, left_hbm, filt_hbm,
    rec, rows_buf, obl_ref, dft_ref, twi_ref, send1, recv1, send2, recv2, lbuf, fbuf, lnat, weights,
    rec_sem, out_sem, s1_sem, r1_sem, s2_sem, r2_sem, ls_sem, lr_sem, fs_sem, fr_sem, fm_sem,
):
    s = lax.axis_index("src")
    r = lax.axis_index("rcv")
    z, xh = r // 2, lax.rem(r, 2)
    xl, y, c = s // 8, lax.rem(s // 2, 4), lax.rem(s, 2)

    def src_of(x, yy, core):
        return x * 8 + lax.rem(yy + 8, 4) * 2 + core

    def rcv_of(zz, x):
        return lax.rem(zz + 16, 8) * 2 + x

    def to_rcv(index):
        return (s, index)

    def to_src(index):
        return (index, r)

    peers = [to_rcv(lax.rem(r + d, NR)) for d in range(1, NR)]
    x_peer = src_of(1 - xl, y, c)
    up, down = src_of(xl, y + 1, c), src_of(xl, y - 1, c)
    mate = src_of(xl, y, 1 - c)
    diag_up, diag_down = src_of(1 - xl, y + 1, c), src_of(1 - xl, y - 1, c)
    peers += [to_src(i) for i in (x_peer, up, down, mate, diag_up, diag_down)]

    barrier = pltpu.get_barrier_semaphore()
    for peer in peers:
        pl.semaphore_signal(barrier, inc=1, device_id=peer, device_id_type=MESH)

    constants = [
        pltpu.make_async_copy(obl_hbm, obl_ref, rec_sem.at[5]),
        pltpu.make_async_copy(dft_hbm, dft_ref, rec_sem.at[6]),
        pltpu.make_async_copy(twi_hbm, twi_ref, rec_sem.at[7]),
    ]
    constants[0].start()
    heads = pltpu.make_async_copy(rec_hbm.at[:, :, pl.ds(0, 8), :], rows_buf, rec_sem.at[4])
    heads.start()
    chunk = ROWS // 4
    loads = []
    for q in range(4):
        load = pltpu.make_async_copy(
            rec_hbm.at[:, pl.ds(4 * q, 4), :, :], rec.at[:, pl.ds(4 * q, 4), :, :], rec_sem.at[q]
        )
        load.start()
        loads.append(load)
    for load in constants[1:]:
        load.start()

    with jax.named_scope("rows"):
        heads.wait()
        for i in range(NR):
            rows = [rows_buf[p, i].astype(F32)[0:1] for p in range(2)]
            send1[i] = jnp.concatenate(rows, axis=0).astype(BF16)

    with jax.named_scope("barrier"):
        pl.semaphore_wait(barrier, len(peers))

    def remote(src, dst, send_sem, recv_sem, device):
        copy = pltpu.make_async_remote_copy(
            src_ref=src, dst_ref=dst, send_sem=send_sem, recv_sem=recv_sem, device_id=device, device_id_type=MESH
        )
        copy.start()

    def drain(buffer, sem, blocks=15):
        pltpu.make_async_copy(buffer.at[pl.ds(0, blocks)], buffer.at[pl.ds(0, blocks)], sem).wait()

    order = [8, 9, 7, 6, 10, 11, 5, 4, 12, 13, 3, 2, 14, 15, 1]
    for d in order:
        other = lax.rem(r + d, NR)
        remote(send1.at[other], recv1.at[r], s1_sem, r1_sem, to_rcv(other))
    recv1[r] = send1[r]

    with jax.named_scope("select"):
        lane = lax.broadcasted_iota(jnp.int32, (1024, 128), 1)
        depth = lax.broadcasted_iota(jnp.int32, (1024, 128), 0)
        pick0 = jnp.where(depth == 64 * lane, 1.0, 0.0).astype(BF16)
        pick1 = jnp.where(depth == 64 * (lane - 16), 1.0, 0.0).astype(BF16)
        pieces = []
        for q in range(4):
            loads[q].wait()
            columns = jnp.dot(rec[0, 4 * q : 4 * q + 4].reshape(chunk, COLS), pick0, preferred_element_type=F32)
            columns += jnp.dot(rec[1, 4 * q : 4 * q + 4].reshape(chunk, COLS), pick1, preferred_element_type=F32)
            turned = columns.T
            pieces.append(turned[0:32])
        local = jnp.concatenate(pieces, axis=1).astype(BF16)
        lbuf[r, 0] = local[0:16]
        lbuf[r, 1] = local[16:32]

    def left_send(owner, h, target):
        remote(lbuf.at[owner, h], lbuf.at[owner, h], ls_sem, lr_sem.at[owner, h], to_rcv(target))

    def left_wait(owner, h):
        pltpu.make_async_copy(lbuf.at[owner, h], lbuf.at[owner, h], lr_sem.at[owner, h]).wait()

    z_up, z_down = rcv_of(z + 1, xh), rcv_of(z - 1, xh)
    far = rcv_of(z, 1 - xh)
    for h in range(2):
        left_send(r, h, far)
    for h in range(2):
        left_send(r, h, z_up)
        left_send(r, h, z_down)

    def left_round(dist, x):
        for h in range(2):
            if dist < 4 or h == 0:
                left_wait(rcv_of(z - dist, x), h)
                if dist + 1 < 4 or (dist + 1 == 4 and h == 0):
                    left_send(rcv_of(z - dist, x), h, z_up)
            if dist < 4 or h == 1:
                left_wait(rcv_of(z + dist, x), h)
                if dist + 1 < 4 or (dist + 1 == 4 and h == 1):
                    left_send(rcv_of(z + dist, x), h, z_down)

    with jax.named_scope("weights"):
        constants[0].wait()
        obl = obl_ref[...] * (1.0 / N)
        hi = obl.astype(BF16)
        rest = obl - hi.astype(F32)
        mid = rest.astype(BF16)
        low = (rest - mid.astype(F32)).astype(BF16)
        parts = jnp.concatenate([hi, mid, low], axis=0)
        column = lax.broadcasted_iota(jnp.int32, (1024, 1024), 0)
        target = lax.broadcasted_iota(jnp.int32, (1024, 1024), 1)
        permute = jnp.where(column == 8 * (target % 128) + target // 128, 1.0, 0.0).astype(BF16)
        moved = jnp.dot(parts, permute, preferred_element_type=F32)
        moved = (moved[0:16] + moved[16:32]) + moved[32:48]
        for h in range(8):
            weights[16 * h : 16 * h + 16, :] = moved[:, 128 * h : 128 * h + 128]

    with jax.named_scope("wait1"):
        drain(recv1, r1_sem)

    with jax.named_scope("left1"):
        left_round(1, xh)

    with jax.named_scope("dft"):
        for load in constants[1:]:
            load.wait()
        rows = recv1[...].astype(F32).reshape(32, 1024)
        x = jnp.concatenate([rows[:, 128 * j : 128 * j + 128] for j in range(8)], axis=0)
        cos, sin = twi_ref[0], twi_ref[1]
        a = jnp.dot(dft_ref[0], x, precision=HIGHEST, preferred_element_type=F32)
        ar, ai = a[0:128], a[128:256]
        b = jnp.concatenate([ar * cos + ai * sin, ai * cos - ar * sin], axis=1)
        b = jnp.dot(b, dft_ref[1], precision=HIGHEST, preferred_element_type=F32)

    with jax.named_scope("far"):
        for h in range(2):
            left_wait(far, h)
            left_send(far, h, z_up)
            left_send(far, h, z_down)

    with jax.named_scope("dft2"):
        w = weights[...]
        b = b * jnp.concatenate([w, w], axis=1)
        b = jnp.dot(b, dft_ref[2], precision=HIGHEST, preferred_element_type=F32)
        ur, ui = b[:, 0:128], b[:, 128:256]
        u = jnp.concatenate([ur * cos - ui * sin, ui * cos + ur * sin], axis=0)
        out = jnp.dot(dft_ref[3], u, precision=HIGHEST, preferred_element_type=F32)

    with jax.named_scope("pack"):
        rounded = out.astype(BF16)
        rho = lax.broadcasted_iota(jnp.int32, (256, 512), 0)
        goal = lax.broadcasted_iota(jnp.int32, (256, 512), 1)
        place = (rho & 1) * 256 + 2 * (8 * ((rho >> 1) & 15) + (rho >> 5))
        sampled = None
        for e in range(2):
            choose = jnp.where(goal == place + e, 1.0, 0.0).astype(BF16)
            got = lax.dot_general(rounded, choose, (((0,), (0,)), ((), ())), preferred_element_type=F32)
            got = got[64 * e : 64 * e + 1]
            sampled = got if sampled is None else sampled + got
        sampled = jnp.concatenate([sampled[:, 0:256], sampled[:, 256:512]], axis=0)
        spread = jnp.concatenate([out[32 * j : 32 * j + 32] for j in range(8)], axis=1)
        for i in range(NR):
            send2[i] = jnp.concatenate([spread[2 * i : 2 * i + 2], sampled], axis=1).astype(BF16)

    for d in order:
        other = lax.rem(r + d, NR)
        remote(send2.at[other], recv2.at[r], s2_sem, r2_sem, to_rcv(other))
    recv2[r] = send2[r]

    with jax.named_scope("left2"):
        left_round(2, xh)
        left_round(1, 1 - xh)

    with jax.named_scope("wait2"):
        drain(recv2, r2_sem)

    with jax.named_scope("unpack"):
        got = recv2[...].astype(F32)
        fbuf[s, 0] = got[:, 0, :].astype(BF16)
        fbuf[s, 1] = got[:, 1, :].astype(BF16)

    def filt_send(owner, h, target):
        remote(fbuf.at[owner, h], fbuf.at[owner, h], fs_sem, fr_sem.at[owner // 2, h], to_src(target))

    def filt_mate(owner, h):
        remote(fbuf.at[owner, h], fbuf.at[owner, h], fs_sem, fm_sem, to_src(mate))

    def filt_wait(owner, h):
        pltpu.make_async_copy(fbuf.at[owner, h], fbuf.at[owner, h], fr_sem.at[owner // 2, h]).wait()

    for h in range(2):
        filt_send(s, h, diag_up if h == 0 else diag_down)
        filt_send(s, h, up if h == 0 else down)
        filt_mate(s, h)
    for h in range(2):
        filt_send(s, h, diag_down if h == 0 else diag_up)
        filt_send(s, h, down if h == 0 else up)
    for h in range(2):
        filt_send(s, h, x_peer)

    def filt_near(x):
        below, above = src_of(x, y - 1, c), src_of(x, y + 1, c)
        filt_wait(below, 0)
        filt_send(below, 0, up)
        filt_mate(below, 0)
        filt_wait(above, 1)
        filt_send(above, 1, down)
        filt_mate(above, 1)
        for owner, h in ((below, 1), (above, 0)):
            filt_wait(owner, h)
            filt_mate(owner, h)

    def filt_last(owner):
        for h in range(2):
            filt_wait(owner, h)
            filt_mate(owner, h)

    with jax.named_scope("left3"):
        left_round(3, xh)
        left_round(2, 1 - xh)

    with jax.named_scope("filt1"):
        filt_near(xl)

    with jax.named_scope("left4"):
        left_round(4, xh)
        left_round(3, 1 - xh)

    with jax.named_scope("filt2"):
        filt_near(1 - xl)

    with jax.named_scope("filt3"):
        filt_last(src_of(xl, y + 2, c))
        filt_last(x_peer)

    with jax.named_scope("filt4"):
        filt_last(src_of(1 - xl, y + 2, c))

    with jax.named_scope("left5"):
        left_round(4, 1 - xh)

    with jax.named_scope("turn"):
        for p in range(2):
            for g in range(2):
                part = lbuf[8 * g : 8 * g + 8, p].reshape(128, ROWS)
                lnat[:, 256 * p + 128 * g : 256 * p + 128 * g + 128] = part.astype(F32).T.astype(BF16)

    left_out = pltpu.make_async_copy(lnat, left_hbm, out_sem.at[0])
    left_out.start()

    with jax.named_scope("store"):
        def filt_store(owner):
            pltpu.make_async_copy(fbuf.at[owner], filt_hbm.at[owner], out_sem.at[1]).start()

        for x in range(2):
            for yy in range(4):
                filt_store(src_of(x, yy, c))
        drain(fbuf, fm_sem, 8)
        for x in range(2):
            for yy in range(4):
                filt_store(src_of(x, yy, 1 - c))

    with jax.named_scope("drain"):
        drain(send1, s1_sem)
        drain(send2, s2_sem)
        drain(lbuf, ls_sem)
        drain(fbuf, fs_sem)
        left_out.wait()
        drain(fbuf, out_sem.at[1], 16)


def gather(recorded, obliquity):
    dft, twiddle = tables()
    hbm = pl.BlockSpec(memory_space=pltpu.HBM)
    anywhere = pl.BlockSpec(memory_space=pl.ANY)
    dma = pltpu.SemaphoreType.DMA
    return pl.pallas_call(
        gather_kernel,
        out_shape=(
            jax.ShapeDtypeStruct((ROWS, 2 * K), BF16),
            jax.ShapeDtypeStruct((NS, 2, 16, WIDE), BF16),
        ),
        in_specs=[hbm] * 4,
        out_specs=(anywhere, anywhere),
        scratch_shapes=[
            pltpu.VMEM((2, 16, 64, COLS), BF16),
            pltpu.VMEM((2, 16, 8, COLS), BF16),
            pltpu.VMEM((16, 1024), F32),
            pltpu.VMEM((4, 256, 256), F32),
            pltpu.VMEM((2, 128, 128), F32),
            pltpu.VMEM((NR, 2, COLS), BF16),
            pltpu.VMEM((NR, 2, COLS), BF16),
            pltpu.VMEM((NR, 2, WIDE), BF16),
            pltpu.VMEM((NR, 2, WIDE), BF16),
            pltpu.VMEM((NR, 2, 16, ROWS), BF16),
            pltpu.VMEM((NS, 2, 16, WIDE), BF16),
            pltpu.VMEM((ROWS, 2 * K), BF16),
            pltpu.VMEM((128, 128), F32),
            dma((8,)),
            dma((2,)),
            dma,
            dma,
            dma,
            dma,
            dma,
            dma((NR, 2)),
            dma,
            dma((NS // 2, 2)),
            dma,
        ],
        compiler_params=pltpu.CompilerParams(
            collective_id=0, has_side_effects=True, vmem_limit_bytes=60 * 2**20
        ),
        name="gather",
    )(recorded.reshape(2, 16, 64, COLS), obliquity, jnp.asarray(dft), jnp.asarray(twiddle))


TC = 256
CHUNK = 256


def update_kernel(rec_ref, left_ref, filt_ref, clip_ref, first_ref, second_ref, left2, scale, minus):
    step = pl.program_id(0)

    @pl.when(step == 0)
    def _():
        for g in range(ROWS // 128):
            clip = jnp.broadcast_to(clip_ref[g : g + 1, :], (128, 128)).T
            scale[128 * g : 128 * g + 128, :] = 1.0 / (clip * clip)

    real_rows = filt_ref[:, 0].reshape(K, TC)
    imag_rows = filt_ref[:, 1].reshape(K, TC)
    minus[...] = -imag_rows
    to_real = jnp.concatenate([real_rows, minus[...]], axis=0)
    to_imag = jnp.concatenate([imag_rows, real_rows], axis=0)

    def limited(left, rows):
        real = jnp.dot(left, to_real, preferred_element_type=F32)
        imag = jnp.dot(left, to_imag, preferred_element_type=F32)
        part = scale[rows, :]
        part = jnp.concatenate([part] * (TC // 128), axis=1)
        limiter = lax.rsqrt(1.0 + (real * real + imag * imag) * part)
        return real * limiter, imag * limiter

    @pl.when(step == 0)
    def _():
        for g in range(ROWS // CHUNK):
            rows = slice(CHUNK * g, CHUNK * g + CHUNK)
            real, imag = limited(left_ref[rows, :], rows)
            left2[rows, 0:K] = (left_ref[rows, 0:K].astype(F32) - real).astype(BF16)
            left2[rows, K : 2 * K] = (left_ref[rows, K : 2 * K].astype(F32) - imag).astype(BF16)

    @pl.when(step > 0)
    def _():
        for g in range(ROWS // CHUNK):
            rows = slice(CHUNK * g, CHUNK * g + CHUNK)
            for left, out in ((left_ref, first_ref), (left2, second_ref)):
                real, imag = limited(left[rows, :], rows)
                out[0, rows, :] = (rec_ref[0, rows, :].astype(F32) - real).astype(BF16)
                out[1, rows, :] = (rec_ref[1, rows, :].astype(F32) - imag).astype(BF16)


def update(recorded, left, filtered, clip_level):
    block = pl.BlockSpec((2, ROWS, TC), lambda i: (0, 0, jnp.maximum(i - 1, 0)))
    once = dict(pipeline_mode=pl.Buffered(1))
    out = jax.ShapeDtypeStruct((2, ROWS, COLS), BF16)
    blocks = COLS // TC
    return pl.pallas_call(
        update_kernel,
        out_shape=(out, out),
        grid=(blocks + 1,),
        in_specs=[
            block,
            pl.BlockSpec((ROWS, 2 * K), lambda i: (0, 0), **once),
            pl.BlockSpec((NS, 2, 16, TC), lambda i: (0, 0, 0, lax.rem(i + blocks, blocks + 1))),
            pl.BlockSpec((ROWS // 128, 128), lambda i: (0, 0), **once),
        ],
        out_specs=(block, block),
        scratch_shapes=[
            pltpu.VMEM((ROWS, 2 * K), BF16),
            pltpu.VMEM((ROWS, 128), F32),
            pltpu.VMEM((K, TC), BF16),
        ],
        compiler_params=pltpu.CompilerParams(vmem_limit_bytes=60 * 2**20),
        name="update",
    )(recorded, left, filtered, clip_level)


def per_device(recorded, obliquity, clip_level):
    left, filtered = gather(recorded, obliquity)
    return update(recorded, left, filtered, clip_level.reshape(ROWS // 128, 128))


def solution(mesh):
    return jax.shard_map(
        per_device,
        mesh=mesh,
        in_specs=(P(None, "src", "rcv"), P(), P("src")),
        out_specs=(P(None, "src", "rcv"), P(None, "src", "rcv")),
        check_vma=False,
    )
```
